32 devices in a mesh: blk: 4 (over y, core), corpus: 8 (over z, x).
Axes of the slice: x: 2, y: 2, z: 4, core: 2. Of those that a mesh axis runs over, the one named last changes fastest.
Arguments:
- states: bfloat16 [8192, 1536], P(('blk', 'corpus')), may hold values from -12 to 12
- table: bfloat16 [8192, 1536], P('corpus'), may hold values from -2.5 to 2.5
- owners: int32 [8192, 4], P(('blk', 'corpus')), may hold values from 0 to 7, as said below
- rows: int32 [8192, 4], P(('blk', 'corpus')), may hold values from 0 to 1023
Outputs:
- loss: float32 [8192], P(('blk', 'corpus'))
- state_grad: bfloat16 [8192, 1536], P(('blk', 'corpus'))
- table_grad: float32 [8192, 1536], P('corpus', 'blk')
The draws below stay inside these ranges and needn't reach their ends.
Inputs may be any that keep to these rules, and one draw needn't show every extreme that they name: `owners`: each state names 4 different shards. Among the 256 states of one device (aligned blocks) no shard is named more than 256 times, and every device names some shard exactly 256 times.
All inputs are finite; a program needn't handle non-finite values.
Results may differ from the reference program's by a relative error of at most 0.012.
Values may be sent and summed in bfloat16 or wider, within the bound.
No kernel may reach another device: no remote copies, remote signals or barrier semaphores. Data moves between devices by JAX's collectives and lax.ppermute only.
A program may use at most 128 MiB of HBM per device.

```python
import math
import jax
import jax.numpy as jnp
from jax import lax

D = 1536
TOP = 4
S_DEV = 256
ROWS_DEV = 1024
CAP = 256
STATES = 8192
ROWS = 8192
N_BLK = 4
N_CORPUS = 8
DEVICES = 32


def id_layout(key):
    shards = N_CORPUS
    spots = S_DEV * TOP
    layout_key = jax.random.fold_in(key, 7001)
    device_keys = jax.random.split(layout_key, DEVICES)
    position = jnp.arange(spots, dtype=jnp.int32)

    def one_device(device_key):
        key_rank, key_order, key_ties, key_weight = jax.random.split(device_key, 4)
        weights = jax.random.randint(key_weight, (shards - 1,), 2, 4).astype(jnp.int32)
        running = jnp.concatenate([jnp.zeros((1,), jnp.int32), jnp.cumsum(weights).astype(jnp.int32)])
        boundary = CAP + (spots - CAP) * running[:shards - 1] // running[shards - 1]
        level = jnp.sum((position[:, None] >= boundary[None, :]).astype(jnp.int32), axis=1)
        shard_of_level = jax.random.permutation(key_rank, shards).astype(jnp.int32)
        layout = shard_of_level[level].reshape(TOP, S_DEV).T
        layout = layout[jax.random.permutation(key_order, S_DEV)]
        ranking = jax.random.randint(key_ties, (S_DEV, TOP), 0, 1 << 20).astype(jnp.int32) * TOP + jnp.arange(TOP, dtype=jnp.int32)[None, :]
        return jnp.take_along_axis(layout, jnp.argsort(ranking, axis=1), axis=1)
    return jax.vmap(one_device)(device_keys).reshape(DEVICES * S_DEV, TOP).astype(jnp.int32)


def row_layout(key):
    hot_count = ROWS_DEV // 32
    key_hot, key_cold, key_coin = jax.random.split(jax.random.fold_in(key, 7002), 3)
    hot_rows = jax.random.randint(key_hot, (STATES, TOP), 0, hot_count)
    cold_rows = jax.random.randint(key_cold, (STATES, TOP), hot_count, ROWS_DEV)
    coin_flip = jax.random.randint(key_coin, (STATES, TOP), 0, 2)
    column_index = jnp.arange(TOP, dtype=jnp.int32)[None, :]
    return jnp.where((coin_flip == 1) & (column_index >= 1), hot_rows, cold_rows).astype(jnp.int32)


def partner_layout(key):
    key_step, key_slot = jax.random.split(jax.random.fold_in(key, 7003), 2)
    state_index = jnp.arange(STATES, dtype=jnp.int32)
    block_index = state_index // (N_CORPUS * S_DEV)
    group_index = state_index // S_DEV % N_CORPUS
    step_size = jax.random.randint(key_step, (STATES,), 1, N_BLK)
    slot_pick = jax.random.randint(key_slot, (STATES,), 0, S_DEV)
    other_block = (block_index + step_size) % N_BLK
    return ((other_block * N_CORPUS + group_index) * S_DEV + slot_pick).astype(jnp.int32)


def table_values(key):
    value_key = jax.random.fold_in(key, 7004)
    return jax.random.truncated_normal(value_key, -2.5, 2.5, (ROWS, D), jnp.float32)


def draw_owners(key, part):
    return id_layout(key)


def draw_rows(key, part):
    return row_layout(key)


def draw_table(key, part):
    return table_values(key).astype(jnp.bfloat16)


def draw_states(key, part):
    owner_ids = id_layout(key)
    row_ids = row_layout(key)
    partner = partner_layout(key)
    premise_ids = (owner_ids * ROWS_DEV + row_ids).astype(jnp.int32)
    values = table_values(key)
    lift = math.log(N_BLK * S_DEV)
    key_pos, key_neg, key_mate, key_base = jax.random.split(jax.random.fold_in(key, 7005), 4)
    pos_shift = jax.random.uniform(key_pos, (STATES,), jnp.float32, -1.0, 2.0)
    neg_shift = jax.random.uniform(key_neg, (STATES, TOP - 1), jnp.float32, -3.5, 1.5)
    mate_shift = jax.random.uniform(key_mate, (STATES,), jnp.float32, -1.0, 2.0)
    base_scale = 11.2 / math.sqrt(D)
    noise = jax.random.truncated_normal(key_base, -2.5, 2.5, (STATES, D), jnp.float32)
    unit_gain = 16.0 / D
    result = base_scale * noise
    result = result + (unit_gain * (lift + pos_shift))[:, None] * jnp.take(values, premise_ids[:, 0], axis=0)
    for column in range(1, TOP):
        result = result + (unit_gain * (lift + neg_shift[:, column - 1]))[:, None] * jnp.take(values, premise_ids[:, column], axis=0)
    mate_ids = jnp.take(premise_ids[:, 0], partner, axis=0)
    result = result + (unit_gain * (lift + mate_shift))[:, None] * jnp.take(values, mate_ids, axis=0)
    return jnp.clip(result, -12.0, 12.0).astype(jnp.bfloat16)


def setup_inputs(seed: int = 0) -> dict:
    key_of = jax.random.split(jax.random.key(seed), 5)
    states = draw_states(jax.random.fold_in(key_of[4], 71), 0)
    table = draw_table(jax.random.fold_in(key_of[4], 71), 0)
    owners = draw_owners(jax.random.fold_in(key_of[4], 71), 0)
    rows = draw_rows(jax.random.fold_in(key_of[4], 71), 0)
    return dict(states=states, table=table, owners=owners, rows=rows)


score_scale = 0.0625


def reference(states, table, owners, rows):
    ids = (owners * ROWS_DEV + rows).astype(jnp.int32)
    group_states = states.reshape(N_BLK, N_CORPUS, S_DEV, D).transpose(1, 0, 2, 3).reshape(N_CORPUS, N_BLK * S_DEV, D)
    group_ids = ids.reshape(N_BLK, N_CORPUS, S_DEV, TOP).transpose(1, 0, 2, 3).reshape(N_CORPUS, N_BLK * S_DEV, TOP)

    def one_group(grad_sum, inputs):
        queries, picks = inputs
        keys = jnp.take(table, picks, axis=0)
        positive = keys[:, 0]
        negative = keys[:, 1:]
        scores = score_scale * jnp.dot(queries, positive.T, preferred_element_type=jnp.float32)
        weight = jnp.exp(scores).astype(jnp.bfloat16)
        hard = score_scale * jnp.einsum("gd,gmd->gm", queries.astype(jnp.float32), negative.astype(jnp.float32))
        hard_weight = jnp.exp(hard).astype(jnp.bfloat16)
        total = jnp.sum(weight.astype(jnp.float32), axis=1) + jnp.sum(hard_weight.astype(jnp.float32), axis=1)
        own = score_scale * jnp.sum(queries.astype(jnp.float32) * positive.astype(jnp.float32), axis=1)
        loss = jnp.log(total) - own
        accum = jnp.dot(weight, positive, preferred_element_type=jnp.float32)
        accum = accum + jnp.einsum("gm,gmd->gd", hard_weight.astype(jnp.float32), negative.astype(jnp.float32))
        state_grad = (score_scale * (accum / total[:, None] - positive.astype(jnp.float32))).astype(jnp.bfloat16)
        prob = (weight.astype(jnp.float32) / total[:, None]).astype(jnp.bfloat16)
        pulled = jnp.dot(prob.T, queries, preferred_element_type=jnp.float32)
        positive_grad = (score_scale * (pulled - queries.astype(jnp.float32))).astype(jnp.bfloat16)
        hard_prob = (hard_weight.astype(jnp.float32) / total[:, None]).astype(jnp.bfloat16)
        negative_grad = (score_scale * hard_prob.astype(jnp.float32)[:, :, None] * queries.astype(jnp.float32)[:, None, :]).astype(jnp.bfloat16)
        row_grads = jnp.concatenate([positive_grad[:, None], negative_grad], axis=1).reshape(-1, D)
        grad_sum = grad_sum + jax.ops.segment_sum(row_grads.astype(jnp.float32), picks.reshape(-1), num_segments=ROWS_DEV * N_CORPUS)
        return grad_sum, (loss, state_grad)

    start = jnp.zeros((ROWS_DEV * N_CORPUS, D), jnp.float32)
    table_grad, (loss, state_grad) = lax.scan(one_group, start, (group_states, group_ids))
    loss = loss.reshape(N_CORPUS, N_BLK, S_DEV).transpose(1, 0, 2).reshape(-1)
    state_grad = state_grad.reshape(N_CORPUS, N_BLK, S_DEV, D).transpose(1, 0, 2, 3).reshape(-1, D)
    return loss, state_grad, table_grad
```

```python
import jax
import jax.numpy as jnp
from jax import lax
from jax.sharding import PartitionSpec as P

score_scale = 0.0625
LINES = 2
LANES = 128
f32 = jnp.float32
bf16 = jnp.bfloat16


class Line:
    def __init__(self, length):
        self.length = length
        self.position = lax.axis_index("corpus") // LINES
        self.rounds = []
        for r in range(1, length):
            right = [(a, a + 1) for a in range(r - 1, length - 1)]
            left = [(a, a - 1) for a in range(1, length - r + 1)]
            one_operand = not ({s for s, _ in right} & {s for s, _ in left})
            one_slot = not ({t for _, t in right} & {t for _, t in left})
            self.rounds.append((r, right, left, one_operand, one_slot))

    def permute(self, value, pairs):
        full = [(s * LINES + i, t * LINES + i) for s, t in pairs for i in range(LINES)]
        return lax.ppermute(value, "corpus", full)

    def places(self):
        a, n = self.position, self.length
        out = [a]
        for r, _, _, _, one_slot in self.rounds:
            from_left = jnp.where(a >= r, a - r, -1)
            from_right = jnp.where(a + r < n, a + r, -1)
            if one_slot:
                out.append(jnp.maximum(from_left, from_right))
            else:
                out += [from_left, from_right]
        return out

    def gather(self, value):
        out = [value]
        lo = hi = value
        for r, right, left, one_operand, one_slot in self.rounds:
            if one_operand:
                both = self.permute(lo, right + left)
                out.append(both)
                lo = hi = both
                continue
            lo, hi = self.permute(lo, right), self.permute(hi, left)
            if one_slot:
                lo = hi = jnp.where(self.position >= r, lo, hi)
                out.append(lo)
            else:
                out += [lo, hi]
        return out

    def scatter(self, part):
        index = 1 + sum(1 if r[4] else 2 for r in self.rounds)
        lo_in = hi_in = both_in = None

        def plus(slot, *arrived):
            total = part(slot)
            for value in arrived:
                if value is not None:
                    total = total + value.astype(f32)
            return total

        def turn(pairs):
            return [(t, s) for s, t in pairs]

        for r, right, left, one_operand, one_slot in reversed(self.rounds):
            if one_slot:
                index -= 1
                both = plus(index, both_in, lo_in, hi_in).astype(bf16)
                lo = hi = both
            else:
                index -= 2
                lo = plus(index, lo_in).astype(bf16)
                hi = plus(index + 1, hi_in).astype(bf16)
            both_in = lo_in = hi_in = None
            if one_operand:
                both_in = self.permute(lo, turn(right) + turn(left))
            else:
                lo_in, hi_in = self.permute(lo, turn(right)), self.permute(hi, turn(left))
        return plus(0, both_in, lo_in, hi_in)


def beside(value):
    size = lax.axis_size("corpus")
    return lax.ppermute(value, "corpus", [(c, c ^ 1) for c in range(size)])


def across(value, bit):
    size = lax.axis_size("blk")
    return lax.ppermute(value, "blk", [(b, b ^ bit) for b in range(size)])


def blk_gather(value):
    size = lax.axis_size("blk")
    out = {0: value}
    bit = size // 2
    while bit:
        out.update({k | bit: across(v, bit) for k, v in out.items()})
        bit //= 2
    return [out[k] for k in range(size)]


def turned(value, k, size):
    step = value.shape[0] // size
    return [value[(j ^ k) * step : ((j ^ k) + 1) * step] for j in range(size)]


def local(states, table, owners, rows):
    state_rows, width = states.shape
    top = owners.shape[1]
    shard_rows = table.shape[0]
    blks = lax.axis_size("blk")
    line = Line(lax.axis_size("corpus") // LINES)
    b = lax.axis_index("blk")
    lane = lax.axis_index("corpus") % LINES
    part = width // blks
    chunk = LANES if part % LANES == 0 else part
    chunks = part // chunk
    group = blks * state_rows

    mine = lax.dynamic_slice_in_dim(table, b * part, part, axis=1)
    slots = [line.gather(mine[:, k * chunk : (k + 1) * chunk]) for k in range(chunks)]

    ids = (owners * shard_rows + rows).astype(jnp.int32).T
    ids = jnp.concatenate(blk_gather(ids), axis=1)
    ids = jnp.concatenate([ids, beside(ids)], axis=1)
    group_states = jnp.concatenate(blk_gather(states), axis=0)
    sliced = [
        lax.dynamic_slice_in_dim(group_states, (b ^ q) * part, part, axis=1) for q in range(blks)
    ]
    near = sliced[0]
    pair_states = jnp.concatenate([near, beside(near)], axis=0)

    places = line.places()
    match, row_of = [], []
    for place in places:
        base = (place * LINES + lane) * shard_rows
        inside = (ids >= base) & (ids < base + shard_rows) & (place >= 0)
        match.append(inside)
        row_of.append(jnp.sum(jnp.where(inside, ids - base + 1, 0), axis=0) - 1)

    positives, picked, hard_part = [], [], []
    order = jnp.arange(shard_rows, dtype=jnp.int32)
    for k in range(chunks):
        cut = pair_states[:, k * chunk : (k + 1) * chunk].astype(f32)
        positive = jnp.zeros((2 * group, chunk), bf16)
        for j in range(len(places)):
            hot = (row_of[j][:, None] == order[None, :]).astype(bf16)
            got = jnp.dot(hot, slots[k][j], preferred_element_type=f32).astype(bf16)
            positive = jnp.where(match[j][0][:, None], got, positive)
            dots = jnp.sum(cut * got.astype(f32), axis=1)
            hard_part.append(jnp.where(match[j], dots[None, :], 0.0))
            picked.append(got)
        positives.append(positive[:group] + beside(positive[group:]))
    hard = sum(hard_part)
    hard = hard[:, :group] + beside(hard[:, group:])
    bit = blks // 2
    while bit:
        other = across(hard, bit)
        step = state_rows
        hard = hard + jnp.concatenate(
            [other[:, (q ^ bit) * step : ((q ^ bit) + 1) * step] for q in range(blks)], axis=1
        )
        bit //= 2
    hard_weight = jnp.exp(score_scale * hard).astype(bf16).astype(f32)
    hard_weight = jnp.where(jnp.arange(top)[:, None] >= 1, hard_weight, 0.0)

    score = jnp.zeros((group, group), f32)
    keys = []
    for k in range(chunks):
        gathered = blk_gather(positives[k])
        full = jnp.concatenate(
            [jnp.concatenate(turned(v, q, blks), axis=0) for q, v in enumerate(gathered)], axis=1
        )
        keys.append(full)
        query = jnp.concatenate([s[:, k * chunk : (k + 1) * chunk] for s in sliced], axis=1)
        score = score + lax.dot_general(
            full, query, (((1,), (1,)), ((), ())), preferred_element_type=f32
        )
    score = score_scale * score
    weight = jnp.exp(score).astype(bf16)
    total = jnp.sum(weight.astype(f32), axis=0) + jnp.sum(hard_weight, axis=0)
    prob = (weight.astype(f32) / total[None, :]).astype(bf16)
    hard_prob = (hard_weight / total[None, :]).astype(bf16)
    pulled = jnp.dot(prob, near, preferred_element_type=f32)
    positive_grad = (score_scale * (pulled - near.astype(f32))).astype(bf16)
    hard_prob = jnp.concatenate([hard_prob, beside(hard_prob)], axis=1).astype(f32)

    grads = []
    for k in range(chunks):
        cols = slice(k * chunk, (k + 1) * chunk)
        pull = positive_grad[:, cols]
        pull = jnp.concatenate([pull, beside(pull)], axis=0)
        wide = score_scale * pair_states[:, cols].astype(f32)

        def share(j, pull=pull, wide=wide):
            scale = jnp.sum(jnp.where(match[j], hard_prob, 0.0), axis=0)
            value = jnp.where(match[j][0][:, None], pull, (scale[:, None] * wide).astype(bf16))
            hot = (order[:, None] == row_of[j][None, :]).astype(bf16)
            return jnp.dot(hot, value, preferred_element_type=f32)

        grads.append(line.scatter(share))
    table_grad = jnp.concatenate(grads, axis=1)

    both_weight = jnp.concatenate([hard_weight, beside(hard_weight)], axis=1)
    shares = []
    for k in range(chunks):
        accum = jnp.zeros((2 * group, chunk), f32)
        for j in range(len(places)):
            scale = jnp.sum(jnp.where(match[j], both_weight, 0.0), axis=0)
            accum = accum + scale[:, None] * picked[k * len(places) + j].astype(f32)
        shares.append(accum)
    shares = jnp.concatenate(shares, axis=1)
    shares = shares[:group] + beside(shares[group:].astype(bf16)).astype(f32)
    shares = shares.astype(bf16)
    mine_weight = weight[:, :state_rows]
    own_total = total[:state_rows]
    pieces = []
    for q in range(blks):
        piece = shares[q * state_rows : (q + 1) * state_rows]
        if q:
            piece = across(piece, q)
        key = jnp.concatenate([keys[k][:, q * chunk : (q + 1) * chunk] for k in range(chunks)], axis=1)
        accum = lax.dot_general(
            mine_weight, key, (((0,), (0,)), ((), ())), preferred_element_type=f32
        ) + piece.astype(f32)
        pieces.append(
            (score_scale * (accum / own_total[:, None] - key[:state_rows].astype(f32))).astype(bf16)
        )
    state_grad = jnp.zeros((state_rows, width), bf16)
    for q in range(blks):
        state_grad = lax.dynamic_update_slice_in_dim(state_grad, pieces[q], (b ^ q) * part, axis=1)
    corner = score[:state_rows, :state_rows]
    spot = jnp.arange(state_rows)
    own = jnp.sum(jnp.where(spot[:, None] == spot[None, :], corner, 0.0), axis=0)
    loss = jnp.log(own_total) - own
    return loss, state_grad, table_grad


def solution(mesh):
    return jax.shard_map(
        local,
        mesh=mesh,
        in_specs=(
            P(("blk", "corpus"), None),
            P("corpus", None),
            P(("blk", "corpus"), None),
            P(("blk", "corpus"), None),
        ),
        out_specs=(P(("blk", "corpus")), P(("blk", "corpus"), None), P("corpus", "blk")),
        check_vma=False,
    )
```

```python
import jax
import jax.numpy as jnp
from jax import lax
from jax.sharding import PartitionSpec as P

score_scale = 0.0625
LINES = 2
LANES = 128
END_SWAP = [(0, 1), (1, 0), (2, 3), (3, 2)]
MIDDLE_SWAP = [(1, 2), (2, 1)]
OUTWARD = [(1, 0), (2, 3)]
INWARD = [(0, 1), (3, 2)]
f32 = jnp.float32
bf16 = jnp.bfloat16


def line_permute(value, pairs):
    full = [(s * LINES + i, t * LINES + i) for s, t in pairs for i in range(LINES)]
    return lax.ppermute(value, "corpus", full)


def swap(value, length, bit):
    return line_permute(value, [(a, a ^ bit) for a in range(length)])


def beside(value):
    size = lax.axis_size("corpus")
    return lax.ppermute(value, "corpus", [(c, c ^ 1) for c in range(size)])


def across(value, bit):
    size = lax.axis_size("blk")
    return lax.ppermute(value, "blk", [(b, b ^ bit) for b in range(size)])


def blk_gather(value):
    size = lax.axis_size("blk")
    out = {0: value}
    bit = size // 2
    while bit:
        out.update({k | bit: across(v, bit) for k, v in out.items()})
        bit //= 2
    return [out[k] for k in range(size)]


def turned(value, k, size):
    step = value.shape[0] // size
    return [value[(j ^ k) * step : ((j ^ k) + 1) * step] for j in range(size)]


def apart(value):
    return lax.optimization_barrier(value)


def after(value, *earlier):
    return lax.optimization_barrier((value, *earlier))[0]


def local(states, table, owners, rows):
    state_rows, width = states.shape
    top = owners.shape[1]
    shard_rows = table.shape[0]
    blks = lax.axis_size("blk")
    length = lax.axis_size("corpus") // LINES
    b = lax.axis_index("blk")
    a = lax.axis_index("corpus") // LINES
    lane = lax.axis_index("corpus") % LINES
    part = width // blks
    short = length == 4
    chunk = LANES if short and part % LANES == 0 else part
    chunks = part // chunk
    group = blks * state_rows
    cols = [slice(k * chunk, (k + 1) * chunk) for k in range(chunks)]

    mine = lax.dynamic_slice_in_dim(table, b * part, part, axis=1)
    ids = (owners * shard_rows + rows).astype(jnp.int32).T
    fresh = states
    if short:
        middle = (a == 1) | (a == 2)
        lead = line_permute(mine[:, :chunk], END_SWAP)
        beyond = line_permute(mine, MIDDLE_SWAP)
        beside_rows = jnp.concatenate([lead, line_permute(mine[:, chunk:], END_SWAP)], axis=1)
        ids, fresh = lax.optimization_barrier((ids, states, lead))[:2]
        third = jnp.where(middle, beyond, line_permute(beyond, OUTWARD))
        last_rows = line_permute(beside_rows, MIDDLE_SWAP)
        early = [mine, after(beside_rows, beyond), third]
        late = []
        for k in range(chunks):
            piece = last_rows[:, cols[k]]
            late.append(jnp.where(middle, piece, line_permute(piece, OUTWARD)))
        places = [a, a ^ 1, jnp.where(a < 2, 2, 1), jnp.where(a < 2, 3, 0)]
    else:
        held, bit = mine, 1
        while bit < length:
            held = jnp.concatenate([held, swap(held, length, bit)], axis=0)
            bit *= 2
        early = [held[j * shard_rows : (j + 1) * shard_rows] for j in range(length)]
        late = []
        places = [a ^ j for j in range(length)]

    ids = jnp.concatenate(blk_gather(ids), axis=1)
    ids = jnp.concatenate([ids, beside(ids)], axis=1)
    near = []
    for q in range(blks):
        piece = lax.dynamic_slice_in_dim(fresh, (b ^ q) * part, part, axis=1)
        near.append(across(piece, q) if q else piece)
    near = jnp.concatenate(near, axis=0)
    pair_states = jnp.concatenate([near, beside(near)], axis=0)
    group_states = jnp.concatenate(blk_gather(after(states, near)), axis=0)
    sliced = [
        lax.dynamic_slice_in_dim(group_states, (b ^ q) * part, part, axis=1) for q in range(blks)
    ]

    match, row_of = [], []
    for place in places:
        base = (place * LINES + lane) * shard_rows
        inside = (ids >= base) & (ids < base + shard_rows)
        match.append(inside)
        row_of.append(jnp.sum(jnp.where(inside, ids - base + 1, 0), axis=0) - 1)
    order = jnp.arange(shard_rows, dtype=jnp.int32)

    def pick(j, rows):
        hot = (row_of[j][:, None] == order[None, :]).astype(bf16)
        return jnp.dot(hot, rows, preferred_element_type=f32).astype(bf16)

    def choose(j, got, positive):
        return jnp.where(match[j][0][:, None], got, positive)

    def dots_of(j, got, cut):
        dots = jnp.sum(cut.astype(f32) * got.astype(f32), axis=1)
        return jnp.where(match[j], dots[None, :], 0.0)

    picked = [pick(j, rows) for j, rows in enumerate(early)]
    positive = jnp.zeros((2 * group, part), bf16)
    hard = 0.0
    for j, got in enumerate(picked):
        positive = choose(j, got, positive)
        hard = hard + dots_of(j, got, pair_states)
    positives, last, came = [], [], []
    for k in range(chunks):
        value = positive[:, cols[k]]
        if late:
            j = len(early)
            rows = after(late[k], came[k - 2]) if k > 1 else late[k]
            last.append(pick(j, rows))
            value = choose(j, last[k], value)
            hard = hard + dots_of(j, last[k], pair_states[:, cols[k]])
        away = value[group:]
        came.append(beside(after(away, came[-1]) if came else away))
        positives.append(value[:group] + came[-1])
    gathered = [blk_gather(positive) for positive in positives]
    half = blks // 2
    hard = hard[:, :group] + beside(after(hard[:, group:], came[-1], gathered[0][half]))
    bit = half
    while bit:
        if bit == half and chunks > 2:
            hard = after(hard, gathered[1][half])
        other = across(hard, bit)
        step = state_rows
        hard = hard + jnp.concatenate(
            [other[:, (q ^ bit) * step : ((q ^ bit) + 1) * step] for q in range(blks)], axis=1
        )
        bit //= 2
    hard_weight = jnp.exp(score_scale * hard).astype(bf16).astype(f32)
    hard_weight = jnp.where(jnp.arange(top)[:, None] >= 1, hard_weight, 0.0)

    score = jnp.zeros((group, group), f32)
    keys = []
    for k in range(chunks):
        full = jnp.concatenate(
            [jnp.concatenate(turned(v, q, blks), axis=0) for q, v in enumerate(gathered[k])], axis=1
        )
        keys.append(full)
        query = jnp.concatenate([s[:, cols[k]] for s in sliced], axis=1)
        score = score + lax.dot_general(
            full, query, (((1,), (1,)), ((), ())), preferred_element_type=f32
        )
    score = score_scale * score
    weight = jnp.exp(score).astype(bf16)
    total = jnp.sum(weight.astype(f32), axis=0) + jnp.sum(hard_weight, axis=0)
    prob = (weight.astype(f32) / total[None, :]).astype(bf16)
    hard_prob = (hard_weight / total[None, :]).astype(bf16)
    far_prob = beside(hard_prob)
    pulled = jnp.dot(prob, near, preferred_element_type=f32)
    positive_grad = (score_scale * (pulled - near.astype(f32))).astype(bf16)
    pulls = []
    for k in range(chunks):
        pull = positive_grad[:, cols[k]]
        pulls.append(jnp.concatenate([pull, beside(after(pull, far_prob) if k else pull)], axis=0))
    pair_prob = jnp.concatenate([hard_prob, far_prob], axis=1).astype(f32)
    wide = score_scale * pair_states.astype(f32)

    def share(j, pull, wide):
        scale = jnp.sum(jnp.where(match[j], pair_prob, 0.0), axis=0)
        value = jnp.where(match[j][0][:, None], pull, (scale[:, None] * wide).astype(bf16))
        hot = (order[:, None] == row_of[j][None, :]).astype(bf16)
        return jnp.dot(hot, value, preferred_element_type=f32)

    pull = jnp.concatenate(pulls, axis=1)
    both_weight = jnp.concatenate([hard_weight, beside(hard_weight)], axis=1)
    if short:
        ends = []
        for k in range(chunks):
            end = share(3, pulls[k], wide[:, cols[k]]).astype(bf16)
            ends.append((end, line_permute(end, INWARD)))
        third = apart(share(2, pull, wide).astype(bf16))
        later = after(pull, ends[-1][1])
        both_weight = after(both_weight, ends[-1][1])
        last_sum = jnp.concatenate([(e.astype(f32) + g.astype(f32)).astype(bf16) for e, g in ends], axis=1)
        inner = line_permute(third, INWARD)
        crossed = line_permute(last_sum, MIDDLE_SWAP)
        beside_sum = apart(share(1, later, wide))
        beside_sum = (beside_sum + crossed.astype(f32)).astype(bf16)
        third = (third.astype(f32) + inner.astype(f32)).astype(bf16)
        table_grad = apart(share(0, later, wide))
        gate = (beside_sum, third)
        table_grad = table_grad + line_permute(beside_sum, END_SWAP).astype(f32)
        table_grad = table_grad + line_permute(third, MIDDLE_SWAP).astype(f32)
    else:
        held = jnp.concatenate([share(j, pull, wide) for j in range(length)], axis=0)
        bit = length // 2
        while bit:
            cut = bit * shard_rows
            held = held[:cut] + swap(held[cut:].astype(bf16), length, bit).astype(f32)
            bit //= 2
        table_grad = held
        gate = ()

    def weighted(j, got):
        scale = jnp.sum(jnp.where(match[j], both_weight, 0.0), axis=0)
        return scale[:, None] * got.astype(f32)

    shares = sum(weighted(j, got) for j, got in enumerate(picked))
    if late:
        shares = shares + weighted(len(early), jnp.concatenate(last, axis=1))
    moved = after(beside(shares[group:].astype(bf16)), *gate)
    shares = (shares[:group] + moved.astype(f32)).astype(bf16)
    mine_weight = weight[:, :state_rows]
    own_total = total[:state_rows]
    pieces = []
    for q in range(blks):
        piece = shares[q * state_rows : (q + 1) * state_rows]
        if q:
            piece = across(piece, q)
        key = jnp.concatenate([key[:, q * chunk : (q + 1) * chunk] for key in keys], axis=1)
        accum = lax.dot_general(
            mine_weight, key, (((0,), (0,)), ((), ())), preferred_element_type=f32
        ) + piece.astype(f32)
        pieces.append(
            (score_scale * (accum / own_total[:, None] - key[:state_rows].astype(f32))).astype(bf16)
        )
    state_grad = jnp.zeros((state_rows, width), bf16)
    for q in range(blks):
        state_grad = lax.dynamic_update_slice_in_dim(state_grad, pieces[q], (b ^ q) * part, axis=1)
    corner = score[:state_rows, :state_rows]
    spot = jnp.arange(state_rows)
    own = jnp.sum(jnp.where(spot[:, None] == spot[None, :], corner, 0.0), axis=0)
    loss = jnp.log(own_total) - own
    return loss, state_grad, table_grad


def solution(mesh):
    return jax.shard_map(
        local,
        mesh=mesh,
        in_specs=(
            P(("blk", "corpus"), None),
            P("corpus", None),
            P(("blk", "corpus"), None),
            P(("blk", "corpus"), None),
        ),
        out_specs=(P(("blk", "corpus")), P(("blk", "corpus"), None), P("corpus", "blk")),
        check_vma=False,
    )
```

```python
import jax
import jax.numpy as jnp
from jax import lax
from jax.experimental.layout import Layout, with_layout_constraint
from jax.sharding import PartitionSpec as P

score_scale = 0.0625
LINES = 2
LANES = 128
END_SWAP = [(0, 1), (1, 0), (2, 3), (3, 2)]
MIDDLE_SWAP = [(1, 2), (2, 1)]
OUTWARD = [(1, 0), (2, 3)]
INWARD = [(0, 1), (3, 2)]
f32 = jnp.float32
bf16 = jnp.bfloat16


def line_permute(value, pairs):
    full = [(s * LINES + i, t * LINES + i) for s, t in pairs for i in range(LINES)]
    return lax.ppermute(value, "corpus", full)


def swap(value, length, bit):
    return line_permute(value, [(a, a ^ bit) for a in range(length)])


def beside(value):
    size = lax.axis_size("corpus")
    return lax.ppermute(value, "corpus", [(c, c ^ 1) for c in range(size)])


def across(value, bit):
    size = lax.axis_size("blk")
    return lax.ppermute(value, "blk", [(b, b ^ bit) for b in range(size)])


def blk_gather(value):
    size = lax.axis_size("blk")
    out = {0: value}
    bit = size // 2
    while bit:
        out.update({k | bit: across(v, bit) for k, v in out.items()})
        bit //= 2
    return [out[k] for k in range(size)]


def turned(value, k, size):
    step = value.shape[0] // size
    return [value[(j ^ k) * step : ((j ^ k) + 1) * step] for j in range(size)]


def rowwise(value):
    return with_layout_constraint(value, Layout(major_to_minor=(0, 1)))


def apart(value):
    return lax.optimization_barrier(value)


def after(value, *earlier):
    return lax.optimization_barrier((value, *earlier))[0]


def local(states, table, owners, rows):
    state_rows, width = states.shape
    top = owners.shape[1]
    shard_rows = table.shape[0]
    blks = lax.axis_size("blk")
    length = lax.axis_size("corpus") // LINES
    b = lax.axis_index("blk")
    a = lax.axis_index("corpus") // LINES
    lane = lax.axis_index("corpus") % LINES
    part = width // blks
    short = length == 4
    chunk = LANES if short and part % LANES == 0 else part
    chunks = part // chunk
    group = blks * state_rows
    cols = [slice(k * chunk, (k + 1) * chunk) for k in range(chunks)]

    mine = lax.dynamic_slice_in_dim(table, b * part, part, axis=1)
    ids = (owners * shard_rows + rows).astype(jnp.int32).T
    fresh = states
    if short:
        middle = (a == 1) | (a == 2)
        lead = line_permute(mine[:, :chunk], END_SWAP)
        beyond = line_permute(mine, MIDDLE_SWAP)
        trail = line_permute(mine[:, chunk:], END_SWAP)
        ids, fresh = lax.optimization_barrier((ids, states, lead))[:2]
        lead_last = line_permute(lead, MIDDLE_SWAP)
        trail_last = line_permute(trail, MIDDLE_SWAP)
        outer = line_permute(beyond, OUTWARD)
        third = jnp.where(middle, beyond, outer)
        beside_rows = jnp.concatenate([lead, after(trail, beyond)], axis=1)
        early = [mine, beside_rows, third]
        wait = [beyond]
        late, moved = [], []
        for k in range(chunks):
            piece = trail_last[:, cols[k - 1]] if k else lead_last
            if k:
                piece = after(piece, outer, *moved[: k - 1])
            moved.append(line_permute(piece, OUTWARD))
            late.append((piece, moved[k]))
        places = [a, a ^ 1, jnp.where(a < 2, 2, 1), jnp.where(a < 2, 3, 0)]
    else:
        held, bit = mine, 1
        while bit < length:
            held = jnp.concatenate([held, swap(held, length, bit)], axis=0)
            bit *= 2
        early = [held[j * shard_rows : (j + 1) * shard_rows] for j in range(length)]
        late, wait = [], []
        places = [a ^ j for j in range(length)]

    ids = jnp.concatenate(blk_gather(ids), axis=1)
    ids = jnp.concatenate([ids, beside(ids)], axis=1)
    near = []
    for q in range(blks):
        piece = lax.dynamic_slice_in_dim(fresh, (b ^ q) * part, part, axis=1)
        near.append(across(piece, q) if q else piece)
    near = jnp.concatenate(near, axis=0)
    pair_states = jnp.concatenate([near, beside(near)], axis=0)
    bit = blks // 2
    met = across(after(states, near, *wait), bit)
    group_states = {0: states, bit: met}
    while bit > 1:
        bit //= 2
        group_states.update({k | bit: across(after(v, met), bit) for k, v in group_states.items()})
    group_states = jnp.concatenate([group_states[k] for k in range(blks)], axis=0)
    sliced = [
        lax.dynamic_slice_in_dim(group_states, (b ^ q) * part, part, axis=1) for q in range(blks)
    ]

    match, row_of = [], []
    for place in places:
        base = (place * LINES + lane) * shard_rows
        inside = (ids >= base) & (ids < base + shard_rows)
        match.append(inside)
        row_of.append(jnp.sum(jnp.where(inside, ids - base + 1, 0), axis=0) - 1)
    order = jnp.arange(shard_rows, dtype=jnp.int32)

    def pick(j, rows):
        hot = (row_of[j][:, None] == order[None, :]).astype(bf16)
        return jnp.dot(hot, rows, preferred_element_type=f32).astype(bf16)

    def choose(j, got, positive):
        return jnp.where(match[j][0][:, None], got, positive)

    def dots_of(j, got, cut):
        dots = jnp.sum(cut.astype(f32) * got.astype(f32), axis=1)
        return jnp.where(match[j], dots[None, :], 0.0)

    picked = [pick(j, rows) for j, rows in enumerate(early)]
    positive = jnp.zeros((2 * group, part), bf16)
    hard = 0.0
    for j, got in enumerate(picked):
        positive = choose(j, got, positive)
        hard = hard + dots_of(j, got, pair_states)
    bases = [positive]
    if late:
        bases = apart([positive[:, c] for c in cols])
    positives, last, came, gathered = [], [], [], []
    for k in range(chunks):
        base, gates = bases[k], ([] if k else [met])
        if late:
            j = len(early)
            piece, swapped, base = lax.optimization_barrier((*late[k], base, *gates))[:3]
            last.append(apart(pick(j, jnp.where(middle, piece, swapped))))
            base = choose(j, last[k], base)
            hard = hard + dots_of(j, last[k], pair_states[:, cols[k]])
        near_rows, away = apart((base[:group], base[group:]))
        came.append(beside(after(away, came[-1]) if came else away))
        positives.append(near_rows + came[-1])
        gathered.append(blk_gather(positives[-1]))
    half = blks // 2
    hard = hard[:, :group] + beside(after(hard[:, group:], came[max(0, chunks - 2)]))
    bit = half
    while bit:
        if bit == half:
            hard = after(hard, gathered[max(0, chunks - 2)][half])
        other = across(hard, bit)
        step = state_rows
        hard = hard + jnp.concatenate(
            [other[:, (q ^ bit) * step : ((q ^ bit) + 1) * step] for q in range(blks)], axis=1
        )
        bit //= 2
    hard_weight = jnp.exp(score_scale * hard).astype(bf16).astype(f32)
    hard_weight = jnp.where(jnp.arange(top)[:, None] >= 1, hard_weight, 0.0)

    score = jnp.zeros((group, group), f32)
    keys = []
    for k in range(chunks):
        full = jnp.concatenate(
            [jnp.concatenate(turned(v, q, blks), axis=0) for q, v in enumerate(gathered[k])], axis=1
        )
        keys.append(full)
        query = jnp.concatenate([s[:, cols[k]] for s in sliced], axis=1)
        score = score + lax.dot_general(
            full, query, (((1,), (1,)), ((), ())), preferred_element_type=f32
        )
    score = score_scale * score
    weight = jnp.exp(score).astype(bf16)
    total = jnp.sum(weight.astype(f32), axis=0) + jnp.sum(hard_weight, axis=0)
    prob = (weight.astype(f32) / total[None, :]).astype(bf16)
    hard_prob = (hard_weight / total[None, :]).astype(bf16)
    far = beside(jnp.concatenate([hard_prob.astype(f32), hard_weight], axis=0))
    far_prob, far_weight = far[:top], far[top:]
    pulled = jnp.dot(prob, near, preferred_element_type=f32)
    positive_grad = (score_scale * (pulled - near.astype(f32))).astype(bf16)
    pulls, far_pulls = [], []
    for k in range(chunks):
        pull = positive_grad[:, cols[k]]
        far_pulls.append(beside(after(pull, far) if k else pull))
        pulls.append(jnp.concatenate([pull, far_pulls[k]], axis=0))
    pair_prob = jnp.concatenate([hard_prob.astype(f32), far_prob], axis=1)
    wide = score_scale * pair_states.astype(f32)

    def share(j, pull, wide):
        scale = jnp.sum(jnp.where(match[j], pair_prob, 0.0), axis=0)
        value = jnp.where(match[j][0][:, None], pull, (scale[:, None] * wide).astype(bf16))
        hot = (order[:, None] == row_of[j][None, :]).astype(bf16)
        return jnp.dot(hot, value, preferred_element_type=f32)

    pull = jnp.concatenate(pulls, axis=1)
    if short:
        ends, crossed = [], []
        for k in range(chunks):
            end = share(3, pulls[k], wide[:, cols[k]]).astype(bf16)
            ends.append(line_permute(end, INWARD))
            both = (end.astype(f32) + ends[k].astype(f32)).astype(bf16)
            crossed.append(line_permute(both, MIDDLE_SWAP))
        third = apart(rowwise(share(2, after(pull, end), wide).astype(bf16)))
        later = after(pull, ends[-1])
        crossed = jnp.concatenate(crossed, axis=1)
        inner = line_permute(third, INWARD)
        beside_sum = apart(rowwise(share(1, later, wide).astype(bf16)))
        beside_sum = (beside_sum.astype(f32) + crossed.astype(f32)).astype(bf16)
        third = (third.astype(f32) + inner.astype(f32)).astype(bf16)
        table_grad = apart(rowwise(share(0, later, wide).astype(bf16))).astype(f32)
        gate = (beside_sum, third)
        table_grad = table_grad + line_permute(beside_sum, END_SWAP).astype(f32)
        table_grad = table_grad + line_permute(third, MIDDLE_SWAP).astype(f32)
    else:
        held = jnp.concatenate([share(j, pull, wide) for j in range(length)], axis=0)
        bit = length // 2
        while bit:
            cut = bit * shard_rows
            held = held[:cut] + swap(held[cut:].astype(bf16), length, bit).astype(f32)
            bit //= 2
        table_grad = held
        gate = ()

    both_weight = jnp.concatenate([hard_weight, far_weight], axis=1)

    def weighted(j, got):
        scale = jnp.sum(jnp.where(match[j], both_weight, 0.0), axis=0)
        return scale[:, None] * got.astype(f32)

    shares = sum(weighted(j, got) for j, got in enumerate(picked))
    if late:
        shares = shares + weighted(len(early), jnp.concatenate(last, axis=1))
    moved = after(beside(after(shares[group:].astype(bf16), far_pulls[-1])), *gate)
    shares = (shares[:group] + moved.astype(f32)).astype(bf16)
    mine_weight = weight[:, :state_rows]
    own_total = total[:state_rows]
    pieces = []
    for q in range(blks):
        piece = shares[q * state_rows : (q + 1) * state_rows]
        if q:
            piece = across(piece, q)
        key = jnp.concatenate([key[:, q * chunk : (q + 1) * chunk] for key in keys], axis=1)
        accum = lax.dot_general(
            mine_weight, key, (((0,), (0,)), ((), ())), preferred_element_type=f32
        ) + piece.astype(f32)
        pieces.append(
            (score_scale * (accum / own_total[:, None] - key[:state_rows].astype(f32))).astype(bf16)
        )
    state_grad = jnp.zeros((state_rows, width), bf16)
    for q in range(blks):
        state_grad = lax.dynamic_update_slice_in_dim(state_grad, pieces[q], (b ^ q) * part, axis=1)
    corner = score[:state_rows, :state_rows]
    spot = jnp.arange(state_rows)
    own = jnp.sum(jnp.where(spot[:, None] == spot[None, :], corner, 0.0), axis=0)
    loss = jnp.log(own_total) - own
    return loss, state_grad, table_grad


def solution(mesh):
    return jax.shard_map(
        local,
        mesh=mesh,
        in_specs=(
            P(("blk", "corpus"), None),
            P("corpus", None),
            P(("blk", "corpus"), None),
            P(("blk", "corpus"), None),
        ),
        out_specs=(P(("blk", "corpus")), P(("blk", "corpus"), None), P("corpus", "blk")),
        check_vma=False,
    )
```

```python
import jax
import jax.numpy as jnp
from jax import lax
from jax.experimental.layout import Layout, with_layout_constraint
from jax.sharding import PartitionSpec as P

score_scale = 0.0625
LINES = 2
LANES = 128
END_SWAP = [(0, 1), (1, 0), (2, 3), (3, 2)]
MIDDLE_SWAP = [(1, 2), (2, 1)]
OUTWARD = [(1, 0), (2, 3)]
INWARD = [(0, 1), (3, 2)]
f32 = jnp.float32
bf16 = jnp.bfloat16


def line_permute(value, pairs):
    full = [(s * LINES + i, t * LINES + i) for s, t in pairs for i in range(LINES)]
    return lax.ppermute(value, "corpus", full)


def swap(value, length, bit):
    return line_permute(value, [(a, a ^ bit) for a in range(length)])


def beside(value):
    size = lax.axis_size("corpus")
    return lax.ppermute(value, "corpus", [(c, c ^ 1) for c in range(size)])


def across(value, bit):
    size = lax.axis_size("blk")
    return lax.ppermute(value, "blk", [(b, b ^ bit) for b in range(size)])


def blk_gather(value):
    size = lax.axis_size("blk")
    out = {0: value}
    bit = size // 2
    while bit:
        out.update({k | bit: across(v, bit) for k, v in out.items()})
        bit //= 2
    return [out[k] for k in range(size)]


def turned(value, k, size):
    step = value.shape[0] // size
    return [value[(j ^ k) * step : ((j ^ k) + 1) * step] for j in range(size)]


def rowwise(value):
    return with_layout_constraint(value, Layout(major_to_minor=(0, 1)))


def apart(value):
    return lax.optimization_barrier(value)


def after(value, *earlier):
    return lax.optimization_barrier((value, *earlier))[0]


def local(states, table, owners, rows):
    state_rows, width = states.shape
    top = owners.shape[1]
    shard_rows = table.shape[0]
    blks = lax.axis_size("blk")
    length = lax.axis_size("corpus") // LINES
    b = lax.axis_index("blk")
    a = lax.axis_index("corpus") // LINES
    lane = lax.axis_index("corpus") % LINES
    part = width // blks
    short = length == 4
    widths = [LANES, part - LANES] if short and part > LANES else [part]
    chunks = len(widths)
    group = blks * state_rows
    starts = [sum(widths[:k]) for k in range(chunks)]
    cols = [slice(at, at + wide) for at, wide in zip(starts, widths)]

    mine = lax.dynamic_slice_in_dim(table, b * part, part, axis=1)
    ids = (owners * shard_rows + rows).astype(jnp.int32).T
    fresh = states
    if short:
        middle = (a == 1) | (a == 2)
        lead = line_permute(mine[:, : widths[0]], END_SWAP)
        beyond = line_permute(mine, MIDDLE_SWAP)
        trail = line_permute(mine[:, widths[0] :], END_SWAP)
        ids, fresh = lax.optimization_barrier((ids, states, lead))[:2]
        lead_last = line_permute(lead, MIDDLE_SWAP)
        trail_last = line_permute(trail, MIDDLE_SWAP)
        outer = line_permute(beyond, OUTWARD)
        third = jnp.where(middle, beyond, outer)
        beside_rows = jnp.concatenate([lead, after(trail, beyond)], axis=1)
        early = [mine, beside_rows, third]
        wait = [beyond]
        late, moved = [], []
        for k in range(chunks):
            piece = trail_last[:, starts[k] - widths[0] :][:, : widths[k]] if k else lead_last
            if k:
                piece = after(piece, outer, *moved[: k - 1])
            moved.append(line_permute(piece, OUTWARD))
            late.append((piece, moved[k]))
        places = [a, a ^ 1, jnp.where(a < 2, 2, 1), jnp.where(a < 2, 3, 0)]
    else:
        held, bit = mine, 1
        while bit < length:
            held = jnp.concatenate([held, swap(held, length, bit)], axis=0)
            bit *= 2
        early = [held[j * shard_rows : (j + 1) * shard_rows] for j in range(length)]
        late, wait = [], []
        places = [a ^ j for j in range(length)]

    ids = jnp.concatenate(blk_gather(ids), axis=1)
    ids = jnp.concatenate([ids, beside(ids)], axis=1)
    near = []
    for q in range(blks):
        piece = lax.dynamic_slice_in_dim(fresh, (b ^ q) * part, part, axis=1)
        near.append(across(piece, q) if q else piece)
    near = jnp.concatenate(near, axis=0)
    pair_states = jnp.concatenate([near, beside(near)], axis=0)
    bit = blks // 2
    met = across(after(states, near, *wait), bit)
    group_states = {0: states, bit: met}
    while bit > 1:
        bit //= 2
        group_states.update({k | bit: across(after(v, met), bit) for k, v in group_states.items()})
    group_states = jnp.concatenate([group_states[k] for k in range(blks)], axis=0)
    sliced = [
        lax.dynamic_slice_in_dim(group_states, (b ^ q) * part, part, axis=1) for q in range(blks)
    ]

    match, row_of = [], []
    for place in places:
        base = (place * LINES + lane) * shard_rows
        inside = (ids >= base) & (ids < base + shard_rows)
        match.append(inside)
        row_of.append(jnp.sum(jnp.where(inside, ids - base + 1, 0), axis=0) - 1)
    order = jnp.arange(shard_rows, dtype=jnp.int32)

    def pick(j, rows):
        hot = (row_of[j][:, None] == order[None, :]).astype(bf16)
        return jnp.dot(hot, rows, preferred_element_type=f32).astype(bf16)

    def choose(j, got, positive):
        return jnp.where(match[j][0][:, None], got, positive)

    def dots_of(j, got, cut):
        dots = jnp.sum(cut.astype(f32) * got.astype(f32), axis=1)
        return jnp.where(match[j], dots[None, :], 0.0)

    picked = [pick(j, rows) for j, rows in enumerate(early)]
    positive = jnp.zeros((2 * group, part), bf16)
    hard = 0.0
    for j, got in enumerate(picked):
        positive = choose(j, got, positive)
        hard = hard + dots_of(j, got, pair_states)
    bases = [positive]
    if late:
        bases = apart([positive[:, c] for c in cols])
    positives, last, came, gathered = [], [], [], []
    for k in range(chunks):
        base, gates = bases[k], ([] if k else [met])
        if late:
            j = len(early)
            piece, swapped, base = lax.optimization_barrier((*late[k], base, *gates))[:3]
            last.append(apart(pick(j, jnp.where(middle, piece, swapped))))
            base = choose(j, last[k], base)
            hard = hard + dots_of(j, last[k], pair_states[:, cols[k]])
        near_rows, away = apart((base[:group], base[group:]))
        came.append(beside(after(away, came[-1]) if came else away))
        positives.append(near_rows + came[-1])
        gathered.append(blk_gather(positives[-1]))
    half = blks // 2
    hard = hard[:, :group] + beside(after(hard[:, group:], gathered[0][half]))
    bit = half
    while bit:
        if bit == half:
            hard = after(hard, gathered[max(0, chunks - 2)][half])
        other = across(hard, bit)
        step = state_rows
        hard = hard + jnp.concatenate(
            [other[:, (q ^ bit) * step : ((q ^ bit) + 1) * step] for q in range(blks)], axis=1
        )
        bit //= 2
    hard_weight = jnp.exp(score_scale * hard).astype(bf16).astype(f32)
    hard_weight = jnp.where(jnp.arange(top)[:, None] >= 1, hard_weight, 0.0)

    score = jnp.zeros((group, group), f32)
    keys = []
    for k in range(chunks):
        full = jnp.concatenate(
            [jnp.concatenate(turned(v, q, blks), axis=0) for q, v in enumerate(gathered[k])], axis=1
        )
        keys.append(full)
        query = jnp.concatenate([s[:, cols[k]] for s in sliced], axis=1)
        score = score + lax.dot_general(
            full, query, (((1,), (1,)), ((), ())), preferred_element_type=f32
        )
    score = score_scale * score
    weight = jnp.exp(score).astype(bf16)
    total = jnp.sum(weight.astype(f32), axis=0) + jnp.sum(hard_weight, axis=0)
    prob = (weight.astype(f32) / total[None, :]).astype(bf16)
    hard_prob = (hard_weight / total[None, :]).astype(bf16)
    far = beside(jnp.concatenate([hard_prob.astype(f32), hard_weight], axis=0))
    far_prob, far_weight = far[:top], far[top:]
    pulled = jnp.dot(prob, near, preferred_element_type=f32)
    positive_grad = (score_scale * (pulled - near.astype(f32))).astype(bf16)
    pulls, far_pulls = [], []
    for k in range(chunks):
        pull = positive_grad[:, cols[k]]
        far_pulls.append(beside(after(pull, far) if k else pull))
        pulls.append(jnp.concatenate([pull, far_pulls[k]], axis=0))
    pair_prob = jnp.concatenate([hard_prob.astype(f32), far_prob], axis=1)
    wide = score_scale * pair_states.astype(f32)

    def share(j, pull, wide):
        scale = jnp.sum(jnp.where(match[j], pair_prob, 0.0), axis=0)
        value = jnp.where(match[j][0][:, None], pull, (scale[:, None] * wide).astype(bf16))
        hot = (order[:, None] == row_of[j][None, :]).astype(bf16)
        return jnp.dot(hot, value, preferred_element_type=f32)

    pull = jnp.concatenate(pulls, axis=1)
    if short:
        ends, crossed = [], []
        for k in range(chunks):
            end = share(3, pulls[k], wide[:, cols[k]]).astype(bf16)
            ends.append(line_permute(end, INWARD))
            both = (end.astype(f32) + ends[k].astype(f32)).astype(bf16)
            crossed.append(line_permute(both, MIDDLE_SWAP))
        third = apart(rowwise(share(2, after(pull, end), wide).astype(bf16)))
        later = after(pull, ends[-1])
        crossed = jnp.concatenate(crossed, axis=1)
        inner = line_permute(third, INWARD)
        beside_sum = apart(rowwise(share(1, later, wide).astype(bf16)))
        beside_sum = (beside_sum.astype(f32) + crossed.astype(f32)).astype(bf16)
        third = (third.astype(f32) + inner.astype(f32)).astype(bf16)
        table_grad = apart(rowwise(share(0, later, wide).astype(bf16))).astype(f32)
        gate = (beside_sum, third)
        table_grad = table_grad + line_permute(beside_sum, END_SWAP).astype(f32)
        table_grad = table_grad + line_permute(third, MIDDLE_SWAP).astype(f32)
    else:
        held = jnp.concatenate([share(j, pull, wide) for j in range(length)], axis=0)
        bit = length // 2
        while bit:
            cut = bit * shard_rows
            held = held[:cut] + swap(held[cut:].astype(bf16), length, bit).astype(f32)
            bit //= 2
        table_grad = held
        gate = ()

    both_weight = jnp.concatenate([hard_weight, far_weight], axis=1)

    def weighted(j, got):
        scale = jnp.sum(jnp.where(match[j], both_weight, 0.0), axis=0)
        return scale[:, None] * got.astype(f32)

    shares = sum(weighted(j, got) for j, got in enumerate(picked))
    if late:
        shares = shares + weighted(len(early), jnp.concatenate(last, axis=1))
    moved = after(beside(after(shares[group:].astype(bf16), far_pulls[-1])), *gate)
    shares = (shares[:group] + moved.astype(f32)).astype(bf16)
    mine_weight = weight[:, :state_rows]
    own_total = total[:state_rows]
    pieces = []
    for q in range(blks):
        piece = shares[q * state_rows : (q + 1) * state_rows]
        if q:
            piece = across(piece, q)
        key = jnp.concatenate([key[:, q * w : (q + 1) * w] for key, w in zip(keys, widths)], axis=1)
        accum = lax.dot_general(
            mine_weight, key, (((0,), (0,)), ((), ())), preferred_element_type=f32
        ) + piece.astype(f32)
        pieces.append(
            (score_scale * (accum / own_total[:, None] - key[:state_rows].astype(f32))).astype(bf16)
        )
    state_grad = jnp.zeros((state_rows, width), bf16)
    for q in range(blks):
        state_grad = lax.dynamic_update_slice_in_dim(state_grad, pieces[q], (b ^ q) * part, axis=1)
    corner = score[:state_rows, :state_rows]
    spot = jnp.arange(state_rows)
    own = jnp.sum(jnp.where(spot[:, None] == spot[None, :], corner, 0.0), axis=0)
    loss = jnp.log(own_total) - own
    return loss, state_grad, table_grad


def solution(mesh):
    return jax.shard_map(
        local,
        mesh=mesh,
        in_specs=(
            P(("blk", "corpus"), None),
            P("corpus", None),
            P(("blk", "corpus"), None),
            P(("blk", "corpus"), None),
        ),
        out_specs=(P(("blk", "corpus")), P(("blk", "corpus"), None), P("corpus", "blk")),
        check_vma=False,
    )
```

```python
import jax
import jax.numpy as jnp
from jax import lax
from jax.experimental.layout import Layout, with_layout_constraint
from jax.sharding import PartitionSpec as P

score_scale = 0.0625
LINES = 2
LANES = 128
END_SWAP = [(0, 1), (1, 0), (2, 3), (3, 2)]
MIDDLE_SWAP = [(1, 2), (2, 1)]
OUTWARD = [(1, 0), (2, 3)]
INWARD = [(0, 1), (3, 2)]
f32 = jnp.float32
bf16 = jnp.bfloat16


def line_permute(value, pairs):
    full = [(s * LINES + i, t * LINES + i) for s, t in pairs for i in range(LINES)]
    return lax.ppermute(value, "corpus", full)


def swap(value, length, bit):
    return line_permute(value, [(a, a ^ bit) for a in range(length)])


def beside(value):
    size = lax.axis_size("corpus")
    return lax.ppermute(value, "corpus", [(c, c ^ 1) for c in range(size)])


def across(value, bit):
    size = lax.axis_size("blk")
    return lax.ppermute(value, "blk", [(b, b ^ bit) for b in range(size)])


def blk_gather(value):
    size = lax.axis_size("blk")
    out = {0: value}
    bit = size // 2
    while bit:
        out.update({k | bit: across(v, bit) for k, v in out.items()})
        bit //= 2
    return [out[k] for k in range(size)]


def turned(value, k, size):
    step = value.shape[0] // size
    return [value[(j ^ k) * step : ((j ^ k) + 1) * step] for j in range(size)]


def rowwise(value):
    return with_layout_constraint(value, Layout(major_to_minor=(0, 1)))


def apart(value):
    return lax.optimization_barrier(value)


def after(value, *earlier):
    return lax.optimization_barrier((value, *earlier))[0]


def local(states, table, owners, rows):
    state_rows, width = states.shape
    top = owners.shape[1]
    shard_rows = table.shape[0]
    blks = lax.axis_size("blk")
    length = lax.axis_size("corpus") // LINES
    b = lax.axis_index("blk")
    a = lax.axis_index("corpus") // LINES
    lane = lax.axis_index("corpus") % LINES
    part = width // blks
    short = length == 4
    widths = [LANES, part - LANES] if short and part > LANES else [part]
    chunks = len(widths)
    group = blks * state_rows
    starts = [sum(widths[:k]) for k in range(chunks)]
    cols = [slice(at, at + wide) for at, wide in zip(starts, widths)]

    mine = lax.dynamic_slice_in_dim(table, b * part, part, axis=1)
    ids = (owners * shard_rows + rows).astype(jnp.int32).T
    fresh = states
    if short:
        middle = (a == 1) | (a == 2)
        lead = line_permute(mine[:, : widths[0]], END_SWAP)
        beyond = line_permute(mine, MIDDLE_SWAP)
        trail = line_permute(mine[:, widths[0] :], END_SWAP)
        ids, fresh = lax.optimization_barrier((ids, states, lead))[:2]
        lead_last = line_permute(lead, MIDDLE_SWAP)
        trail_last = line_permute(trail, MIDDLE_SWAP)
        outer = line_permute(beyond, OUTWARD)
        third = jnp.where(middle, beyond, outer)
        beside_rows = jnp.concatenate([lead, after(trail, beyond)], axis=1)
        early = [mine, beside_rows, third]
        wait = [beyond]
        late, moved = [], []
        for k in range(chunks):
            piece = trail_last[:, starts[k] - widths[0] :][:, : widths[k]] if k else lead_last
            if k:
                piece = after(piece, outer, *moved[: k - 1])
            moved.append(line_permute(piece, OUTWARD))
            late.append((piece, moved[k]))
        places = [a, a ^ 1, jnp.where(a < 2, 2, 1), jnp.where(a < 2, 3, 0)]
    else:
        held, bit = mine, 1
        while bit < length:
            held = jnp.concatenate([held, swap(held, length, bit)], axis=0)
            bit *= 2
        early = [held[j * shard_rows : (j + 1) * shard_rows] for j in range(length)]
        late, wait = [], []
        places = [a ^ j for j in range(length)]

    ids = jnp.concatenate(blk_gather(ids), axis=1)
    ids = jnp.concatenate([ids, beside(ids)], axis=1)
    near = []
    for q in range(blks):
        piece = lax.dynamic_slice_in_dim(fresh, (b ^ q) * part, part, axis=1)
        near.append(across(piece, q) if q else piece)
    near = jnp.concatenate(near, axis=0)
    pair_states = jnp.concatenate([near, beside(near)], axis=0)
    bit = blks // 2
    met = across(after(states, near, *wait), bit)
    group_states = {0: states, bit: met}
    while bit > 1:
        bit //= 2
        group_states.update({k | bit: across(after(v, met), bit) for k, v in group_states.items()})
    group_states = jnp.concatenate([group_states[k] for k in range(blks)], axis=0)
    sliced = [
        lax.dynamic_slice_in_dim(group_states, (b ^ q) * part, part, axis=1) for q in range(blks)
    ]

    match, row_of = [], []
    for place in places:
        base = (place * LINES + lane) * shard_rows
        inside = (ids >= base) & (ids < base + shard_rows)
        match.append(inside)
        row_of.append(jnp.sum(jnp.where(inside, ids - base + 1, 0), axis=0) - 1)
    order = jnp.arange(shard_rows, dtype=jnp.int32)

    def pick(j, rows):
        hot = (row_of[j][:, None] == order[None, :]).astype(bf16)
        return jnp.dot(hot, rows, preferred_element_type=f32).astype(bf16)

    def choose(j, got, positive):
        return jnp.where(match[j][0][:, None], got, positive)

    def dots_of(j, got, cut):
        dots = jnp.sum(cut.astype(f32) * got.astype(f32), axis=1)
        return jnp.where(match[j], dots[None, :], 0.0)

    picked = [pick(j, rows) for j, rows in enumerate(early)]
    positive = jnp.zeros((2 * group, part), bf16)
    hard = 0.0
    for j, got in enumerate(picked):
        positive = choose(j, got, positive)
        hard = hard + dots_of(j, got, pair_states)
    bases = [positive]
    if late:
        bases = apart([positive[:, c] for c in cols])
    positives, last, came, gathered = [], [], [], []
    for k in range(chunks):
        base, gates = bases[k], ([] if k else [met])
        if late:
            j = len(early)
            piece, swapped, base = lax.optimization_barrier((*late[k], base, *gates))[:3]
            last.append(apart(pick(j, jnp.where(middle, piece, swapped))))
            base = choose(j, last[k], base)
            hard = hard + dots_of(j, last[k], pair_states[:, cols[k]])
        near_rows, away = apart((base[:group], base[group:]))
        came.append(beside(after(away, came[-1]) if came else away))
        positives.append(near_rows + came[-1])
        gathered.append(blk_gather(positives[-1]))
    half = blks // 2
    hard = hard[:, :group] + beside(after(hard[:, group:], gathered[0][half]))
    bit = half
    while bit:
        if bit == half:
            hard = after(hard, gathered[max(0, chunks - 2)][half])
        other = across(hard, bit)
        step = state_rows
        hard = hard + jnp.concatenate(
            [other[:, (q ^ bit) * step : ((q ^ bit) + 1) * step] for q in range(blks)], axis=1
        )
        bit //= 2
    hard_weight = jnp.exp(score_scale * hard).astype(bf16).astype(f32)
    hard_weight = jnp.where(jnp.arange(top)[:, None] >= 1, hard_weight, 0.0)

    score = jnp.zeros((group, group), f32)
    keys = []
    for k in range(chunks):
        full = jnp.concatenate(
            [jnp.concatenate(turned(v, q, blks), axis=0) for q, v in enumerate(gathered[k])], axis=1
        )
        keys.append(full)
        query = jnp.concatenate([s[:, cols[k]] for s in sliced], axis=1)
        score = score + lax.dot_general(
            full, query, (((1,), (1,)), ((), ())), preferred_element_type=f32
        )
    score = score_scale * score
    weight = jnp.exp(score).astype(bf16)
    total = jnp.sum(weight.astype(f32), axis=0) + jnp.sum(hard_weight, axis=0)
    prob = (weight.astype(f32) / total[None, :]).astype(bf16)
    hard_prob = (hard_weight / total[None, :]).astype(bf16)
    far = beside(jnp.concatenate([hard_prob.astype(f32), hard_weight], axis=0))
    far_prob, far_weight = far[:top], far[top:]
    pulled = jnp.dot(prob, near, preferred_element_type=f32)
    positive_grad = (score_scale * (pulled - near.astype(f32))).astype(bf16)
    pulls, far_pulls = [], []
    for k in range(chunks):
        pull = positive_grad[:, cols[k]]
        far_pulls.append(beside(after(pull, far) if k else pull))
        pulls.append(jnp.concatenate([pull, far_pulls[k]], axis=0))
    pair_prob = jnp.concatenate([hard_prob.astype(f32), far_prob], axis=1)
    wide = score_scale * pair_states.astype(f32)

    def share(j, pull, wide):
        scale = jnp.sum(jnp.where(match[j], pair_prob, 0.0), axis=0)
        value = jnp.where(match[j][0][:, None], pull, (scale[:, None] * wide).astype(bf16))
        hot = (order[:, None] == row_of[j][None, :]).astype(bf16)
        return jnp.dot(hot, value, preferred_element_type=f32)

    pull = jnp.concatenate(pulls, axis=1)
    if short:
        ends, crossed = [], []
        for k in range(chunks):
            end = share(3, pulls[k], wide[:, cols[k]]).astype(bf16)
            ends.append(line_permute(end, INWARD))
            both = (end.astype(f32) + ends[k].astype(f32)).astype(bf16)
            crossed.append(line_permute(both, MIDDLE_SWAP))
        third = apart(rowwise(share(2, after(pull, end), wide).astype(bf16)))
        later = after(pull, ends[-1])
        crossed = jnp.concatenate(crossed, axis=1)
        inner = line_permute(third, INWARD)
        beside_sum = apart(rowwise(share(1, later, wide).astype(bf16)))
        beside_sum = (beside_sum.astype(f32) + crossed.astype(f32)).astype(bf16)
        third = (third.astype(f32) + inner.astype(f32)).astype(bf16)
        table_grad = apart(rowwise(share(0, later, wide).astype(bf16))).astype(f32)
        beside_sum, third = apart((beside_sum, third))
        gate = (beside_sum, third)
        table_grad = table_grad + line_permute(beside_sum, END_SWAP).astype(f32)
        table_grad = table_grad + line_permute(third, MIDDLE_SWAP).astype(f32)
    else:
        held = jnp.concatenate([share(j, pull, wide) for j in range(length)], axis=0)
        bit = length // 2
        while bit:
            cut = bit * shard_rows
            held = held[:cut] + swap(held[cut:].astype(bf16), length, bit).astype(f32)
            bit //= 2
        table_grad = held
        gate = ()

    both_weight = jnp.concatenate([hard_weight, far_weight], axis=1)

    def weighted(j, got):
        scale = jnp.sum(jnp.where(match[j], both_weight, 0.0), axis=0)
        return scale[:, None] * got.astype(f32)

    shares = sum(weighted(j, got) for j, got in enumerate(picked))
    if late:
        shares = shares + weighted(len(early), jnp.concatenate(last, axis=1))
    moved = after(beside(after(shares[group:].astype(bf16), far_pulls[-1])), *gate)
    shares = (shares[:group] + moved.astype(f32)).astype(bf16)
    mine_weight = weight[:, :state_rows]
    own_total = total[:state_rows]
    pieces = []
    for q in range(blks):
        piece = shares[q * state_rows : (q + 1) * state_rows]
        if q:
            piece = across(piece, q)
        key = jnp.concatenate([key[:, q * w : (q + 1) * w] for key, w in zip(keys, widths)], axis=1)
        accum = lax.dot_general(
            mine_weight, key, (((0,), (0,)), ((), ())), preferred_element_type=f32
        ) + piece.astype(f32)
        pieces.append(
            (score_scale * (accum / own_total[:, None] - key[:state_rows].astype(f32))).astype(bf16)
        )
    state_grad = jnp.zeros((state_rows, width), bf16)
    for q in range(blks):
        state_grad = lax.dynamic_update_slice_in_dim(state_grad, pieces[q], (b ^ q) * part, axis=1)
    corner = score[:state_rows, :state_rows]
    spot = jnp.arange(state_rows)
    own = jnp.sum(jnp.where(spot[:, None] == spot[None, :], corner, 0.0), axis=0)
    loss = jnp.log(own_total) - own
    return loss, state_grad, table_grad


def solution(mesh):
    return jax.shard_map(
        local,
        mesh=mesh,
        in_specs=(
            P(("blk", "corpus"), None),
            P("corpus", None),
            P(("blk", "corpus"), None),
            P(("blk", "corpus"), None),
        ),
        out_specs=(P(("blk", "corpus")), P(("blk", "corpus"), None), P("corpus", "blk")),
        check_vma=False,
    )
```
